32 devices in a mesh: group: 2 (over y), mrow: 4 (over z), mcol: 2 (over x), sub: 2 (over core).
Axes of the slice: x: 2, y: 2, z: 4, core: 2. Of those that a mesh axis runs over, the one named last changes fastest.
Arguments:
- tokens: bfloat16 [1024, 6144], P(('group', 'mrow'), ('mcol', 'sub')), parts along dimension 0, may hold values from -8 to 8
- ln_gain: float32 [6144], P(('mcol', 'sub')), may hold values from 0.1 to 1.9
- w_in: bfloat16 [6144, 24576], P(('mcol', 'sub'), 'mrow'), may hold values from -0.078125 to 0.078125
- b_in: float32 [24576], P('mrow'), may hold values from -3 to 3
- w_out: bfloat16 [24576, 6144], P('mrow', ('mcol', 'sub')), may hold values from -0.0390625 to 0.0390625
- b_out: float32 [6144], replicated, may hold values from -0.6 to 0.6
- captions: bfloat16 [2048, 6144], P(('group', 'mrow', 'mcol', 'sub')), parts along dimension 0, may hold values from -6 to 6
- pairs: int32 [2048], P(('group', 'mrow', 'mcol', 'sub')), parts along dimension 0, may hold values from 0 to 1
Outputs:
- scores: float32 [2048], P(('group', 'mrow', 'mcol', 'sub')), parts along dimension 0
The draws below stay inside these ranges and needn't reach their ends.
There are 2 independent parts, one for each index of `group`. The reference program is written for one: setup_inputs(seed, part) draws one part's arguments, and reference() takes and returns one part's arrays. A program takes and returns all parts, laid end to end along the dimension named above; an argument that names none is the same for every part. Nothing has to cross between parts.
All inputs are finite; a program needn't handle non-finite values.
Results may differ from the reference program's by a relative error of at most 0.0065.
Values may be sent and summed in bfloat16 or wider, within the bound.
A program may use at most 128 MiB of HBM per device.

```python
import jax
import jax.numpy as jnp
from jax import lax

D = 6144
FF = 24576
PATCHES = 256
IMAGES = 2
TOKENS = 512
CAPTIONS = 1024
N_MCOL = 2
N_SUB = 2


def draw_tokens(key, part):
    first, second = jax.random.split(jax.random.fold_in(key, 11), 2)
    common = jax.random.normal(first, (IMAGES, 1, D), jnp.float32)
    noise = jax.random.normal(second, (IMAGES, PATCHES, D), jnp.float32)
    values = 0.8 * common + 0.6 * noise
    values = jnp.clip(values, -8.0, 8.0)
    return values.reshape(IMAGES * PATCHES, D).astype(jnp.bfloat16)


def plant(result, key, least, top_value):
    longest = result.shape.index(max(result.shape))
    spots = []
    for shift in (0, 1):
        where = [jax.random.randint(jax.random.fold_in(key, axis), (), 0, length) for axis, length in enumerate(result.shape)]
        where[longest] = (where[longest] + shift) % result.shape[longest]
        spots.append(tuple(where))
    return result.at[spots[0]].set(least).at[spots[1]].set(top_value)


def levels(key, shape, cuts, smallest, largest):
    factor_of = 1.0
    for dim, shards_of in cuts:
        heights = jax.random.uniform(jax.random.fold_in(jax.random.fold_in(key, 6), dim), (shards_of,), jnp.float32, smallest / len(cuts), largest / len(cuts))
        factor_of = factor_of * jnp.repeat(jnp.exp(heights), shape[dim] // shards_of).reshape((-1,) + (1,) * (len(shape) - 1 - dim))
    return factor_of


def scatter_about(own_key, dims, width, most, cuts=(), held_as=jnp.bfloat16):
    values = width * jax.random.normal(own_key, dims, jnp.float32)
    if cuts:
        values = values * levels(own_key, dims, cuts, -0.22, 0.18)
    return jnp.clip(values, -most, most).astype(held_as)


def setup_inputs(seed: int = 0, part: int = 0) -> dict:
    key_list = jax.random.split(jax.random.key(seed), 9)
    part_splits = jax.random.split(jax.random.fold_in(key_list[8], part), 9)
    return {
        "tokens": draw_tokens(jax.random.fold_in(jax.random.fold_in(key_list[8], part), 71), part),
        "ln_gain": jnp.clip(1.0 + 0.18 * jax.random.normal(key_list[1], (D,), jnp.float32), 0.1, 1.9),
        "w_in": scatter_about(key_list[2], (D, FF), D ** -0.5, 0.078125, ((0, 4), (1, 4))),
        "b_in": scatter_about(key_list[3], (FF,), 0.5, 3.0, ((0, 4),), jnp.float32),
        "w_out": scatter_about(key_list[4], (FF, D), FF ** -0.5, 0.0390625, ((0, 4), (1, 4))),
        "b_out": scatter_about(key_list[5], (D,), 0.1, 0.6, (), jnp.float32),
        "captions": scatter_about(part_splits[6], (CAPTIONS, D), 1.0, 6.0, ((0, 16),)),
        "pairs": plant(jax.random.randint(part_splits[7], (CAPTIONS,), 0, IMAGES), jax.random.fold_in(part_splits[7], 1), 0, IMAGES - 1).astype(jnp.int32),
    }


def reference(tokens, ln_gain, w_in, b_in, w_out, b_out, captions, pairs):
    values = tokens.astype(jnp.float32)
    average = lax.optimization_barrier(jnp.mean(values, axis=1, keepdims=True))
    variance = lax.optimization_barrier(jnp.mean(values * values, axis=1, keepdims=True)) - average * average
    normed = ((values - average) * lax.rsqrt(variance + 1e-06) * ln_gain[None, :]).astype(jnp.bfloat16)
    blocks = N_MCOL * N_SUB
    block_width = D // blocks

    def add_block(index, total):
        offset = index.astype(jnp.int32) * block_width
        segment = lax.dynamic_slice_in_dim(normed, offset, block_width, 1)
        weights = lax.dynamic_slice_in_dim(w_in, offset, block_width, 0)
        partial_value = jnp.dot(segment, weights, preferred_element_type=jnp.float32).astype(jnp.bfloat16)
        partial_value = lax.optimization_barrier(partial_value)
        return total + partial_value.astype(jnp.float32)
    preact = lax.fori_loop(0, blocks, add_block, jnp.zeros((TOKENS, FF), jnp.float32))
    preact = preact + b_in[None, :]
    hidden = jax.nn.gelu(preact, approximate=True).astype(jnp.bfloat16)
    pooled_hidden = lax.optimization_barrier(jnp.sum(hidden.astype(jnp.float32).reshape(IMAGES, PATCHES, FF), axis=1)) / PATCHES
    mixed = jnp.dot(pooled_hidden, w_out.astype(jnp.float32), precision=lax.Precision.HIGHEST)
    pooled = lax.optimization_barrier(jnp.sum(values.reshape(IMAGES, PATCHES, D), axis=1)) / PATCHES + mixed + b_out[None, :]
    embedding = (pooled * lax.rsqrt(lax.optimization_barrier(jnp.mean(pooled * pooled, axis=1, keepdims=True)) + 1e-06)).astype(jnp.bfloat16)
    similar = jnp.dot(captions, embedding.T, preferred_element_type=jnp.float32)
    chosen = pairs[:, None] == jnp.arange(IMAGES, dtype=jnp.int32)[None, :]
    picked = lax.optimization_barrier(jnp.sum(jnp.where(chosen, similar, 0.0), axis=1))
    text_vals = captions.astype(jnp.float32)
    text_scale = lax.rsqrt(lax.optimization_barrier(jnp.mean(text_vals * text_vals, axis=1)) + 1e-06)
    return 100.0 * picked * text_scale / D
```

```python
import functools

import jax
import jax.numpy as jnp
from jax import lax
from jax.experimental import pallas as pl
from jax.experimental.pallas import tpu as pltpu
from jax.sharding import PartitionSpec as P

MESH = pl.DeviceIdType.MESH

D = 6144
PATCHES = 256
IMAGES = 2


def image_table(first_row, count):
    positions = first_row + jnp.arange(count, dtype=jnp.int32)
    return (positions[None, :] // PATCHES == jnp.arange(IMAGES, dtype=jnp.int32)[:, None]).astype(
        jnp.bfloat16
    )


def plain(tokens, ln_gain, w_in, b_in, w_out, b_out, captions, pairs):
    values = tokens.astype(jnp.float32)
    totals, squares = lax.psum(
        (jnp.sum(values, axis=1), jnp.sum(values * values, axis=1)), ("mcol", "sub")
    )
    average = totals / D
    variance = squares / D - average * average
    normed = (
        (values - average[:, None]) * lax.rsqrt(variance + 1e-06)[:, None] * ln_gain[None, :]
    ).astype(jnp.bfloat16)
    gathered = lax.all_gather(normed, "mrow", axis=0, tiled=True)
    rows_local = tokens.shape[0]
    columns = tokens.shape[1]
    col_index = lax.axis_index(("mcol", "sub"))
    row_index = lax.axis_index("mrow")
    resid_pool = jnp.dot(
        image_table(row_index * rows_local, rows_local), tokens, preferred_element_type=jnp.float32
    )
    empty = jnp.zeros((IMAGES, D), jnp.float32)
    offset = col_index * columns
    out_weights = w_out.astype(jnp.float32)
    full_preact = jnp.dot(gathered, w_in, preferred_element_type=jnp.float32)
    preact = lax.psum_scatter(
        full_preact.astype(jnp.bfloat16), ("mcol", "sub"), scatter_dimension=1, tiled=True
    ).astype(jnp.float32)
    units = preact.shape[1]
    unit_bias = lax.dynamic_slice_in_dim(b_in, col_index * units, units, 0)
    hidden = jax.nn.gelu(preact + unit_bias[None, :], approximate=True).astype(jnp.bfloat16)
    local_pool = jnp.dot(
        image_table(0, hidden.shape[0]), hidden, preferred_element_type=jnp.float32
    )
    pooled_hidden = lax.all_gather(local_pool, ("mcol", "sub"), axis=1, tiled=True) / PATCHES
    mixed = jnp.dot(pooled_hidden, out_weights, precision=lax.Precision.HIGHEST)
    placed = lax.dynamic_update_slice(empty, resid_pool / PATCHES + mixed, (0, offset))
    pooled = lax.psum(placed, ("mrow", "mcol", "sub")) + b_out[None, :]
    embedding = (
        pooled * lax.rsqrt(jnp.mean(pooled * pooled, axis=1, keepdims=True) + 1e-06)
    ).astype(jnp.bfloat16)
    similar = jnp.dot(captions, embedding.T, preferred_element_type=jnp.float32)
    chosen = pairs[:, None] == jnp.arange(IMAGES, dtype=jnp.int32)[None, :]
    picked = jnp.sum(jnp.where(chosen, similar, 0.0), axis=1)
    text_vals = captions.astype(jnp.float32)
    text_scale = lax.rsqrt(jnp.mean(text_vals * text_vals, axis=1) + 1e-06)
    return 100.0 * picked * text_scale / D


def column_tile(width):
    return next(t for t in (1536, 768, 512, 384, 256, 128) if width % t == 0)


def unit_tile(width):
    return next(t for t in (512, 256, 384, 128) if width % t == 0)


def kernel(
    sizes,
    tokens_hbm, gain_hbm, w_in_hbm, b_in_hbm, w_out_hbm, b_out_hbm, captions_hbm, pairs_hbm,
    out_ref,
    x_all, normed, w_in_v, w_out_v, captions_v, to_sub, from_sub, kept, to_col, from_col, own,
    gain_v, b_in_v, b_out_v, pairs_v, stats, row_stats, pool_all, acc_v, mixed_all, pooled_all,
    local_sem, w_sem,
    z_send, z_recv, stat_send, stat_recv, rows_send, rows_recv,
    sub_send, sub_recv, col_send, col_recv,
    pool_send, pool_recv, mixed_send, mixed_recv, pooled_send, pooled_recv,
):
    n_r, n_c, n_s = sizes
    n_q = n_c * n_s
    g = lax.axis_index("group")
    r = lax.axis_index("mrow")
    c = lax.axis_index("mcol")
    s = lax.axis_index("sub")
    oc, os = 1 - c, 1 - s
    q = c * n_s + s
    rows, depth = x_all.shape[1], x_all.shape[2]
    tiles, ut = own.shape[1], own.shape[3]
    units = tiles * ut
    features = depth * n_q
    n_caps = captions_v.shape[0]

    def peer_q(k):
        pc, ps = (oc if k & 2 else c), (os if k & 1 else s)
        return pc * n_s + ps, (g, r, pc, ps)

    def peer_r(k):
        other = lax.rem(r + k, n_r)
        return other, (g, other, c, s)

    quarters = (oc * n_s + os, oc * n_s + s, c * n_s + os, c * n_s + s)

    def w_in_copy(j, t):
        start = pl.multiple_of(quarters[j] * units + t * ut, 128)
        return pltpu.make_async_copy(
            w_in_hbm.at[:, pl.ds(start, ut)], w_in_v.at[j, t], w_sem.at[j, t])

    tokens_copy = pltpu.make_async_copy(tokens_hbm, x_all.at[r], local_sem.at[0])
    w_out_copy = pltpu.make_async_copy(w_out_hbm, w_out_v, local_sem.at[1])
    captions_copy = pltpu.make_async_copy(captions_hbm, captions_v, local_sem.at[2])
    gain_copy = pltpu.make_async_copy(gain_hbm, gain_v, local_sem.at[3])
    b_in_copy = pltpu.make_async_copy(
        b_in_hbm.at[:, pl.ds(pl.multiple_of(q * units, 128), units)], b_in_v, local_sem.at[4])
    b_out_copy = pltpu.make_async_copy(
        b_out_hbm.at[:, pl.ds(pl.multiple_of(q * depth, 128), depth)], b_out_v, local_sem.at[5])
    pairs_copy = pltpu.make_async_copy(pairs_hbm, pairs_v, local_sem.at[6])
    tokens_copy.start()

    barrier = pltpu.get_barrier_semaphore()
    for k in range(1, n_q):
        pl.semaphore_signal(barrier, inc=1, device_id=peer_q(k)[1], device_id_type=MESH)

    @pl.when(r > 0)
    def _():
        pl.semaphore_signal(barrier, inc=1, device_id=(g, r - 1, c, s), device_id_type=MESH)

    @pl.when(r + 1 < n_r)
    def _():
        pl.semaphore_signal(barrier, inc=1, device_id=(g, r + 1, c, s), device_id_type=MESH)

    gain_copy.start()
    tokens_copy.wait()
    for pair in (0, 2):
        for t in range(tiles):
            w_in_copy(pair, t).start()
            w_in_copy(pair + 1, t).start()
    b_in_copy.start()
    b_out_copy.start()
    pairs_copy.start()

    ct = column_tile(depth)
    total = jnp.zeros((rows, 1), jnp.float32)
    squares = jnp.zeros((rows, 1), jnp.float32)
    for start in range(0, depth, ct):
        part = x_all[r, :, start : start + ct].astype(jnp.float32)
        total += jnp.sum(part, axis=1, keepdims=True)
        squares += jnp.sum(part * part, axis=1, keepdims=True)
    lane = lax.broadcasted_iota(jnp.int32, (rows, 128), 1)
    both = jnp.where(lane == 0, total, jnp.where(lane == 1, squares, 0.0))
    stats[q] = jnp.transpose(both)[:8, :]

    neighbours = jnp.where(r > 0, 1, 0) + jnp.where(r + 1 < n_r, 1, 0)
    pl.semaphore_wait(barrier, n_q - 1 + neighbours)

    def q_copy(src, dst, send, recv, k):
        return pltpu.make_async_remote_copy(
            src_ref=src, dst_ref=dst, send_sem=send, recv_sem=recv,
            device_id=peer_q(k)[1], device_id_type=MESH)

    def stat_copy(k, slot):
        return q_copy(stats.at[slot], stats.at[slot], stat_send.at[k], stat_recv.at[k], k)

    for k in range(n_q - 1, 0, -1):
        stat_copy(k, q).start()

    def relay(ref, send, recv, way, distance, block):
        towards = r + 1 if way == 0 else r - 1
        return pltpu.make_async_remote_copy(
            src_ref=ref.at[block], dst_ref=ref.at[block], send_sem=send.at[way, distance],
            recv_sem=recv.at[way, distance + 1], device_id=(g, towards, c, s), device_id_type=MESH)

    def relay_arrival(ref, send, recv, way, distance, block):
        return pltpu.make_async_remote_copy(
            src_ref=ref.at[block], dst_ref=ref.at[block], send_sem=send.at[way, 0],
            recv_sem=recv.at[way, distance], device_id=(g, r, c, s), device_id_type=MESH)

    token_relay = (x_all, z_send, z_recv)
    rows_relay = (row_stats, rows_send, rows_recv)

    def forward(what, way, distance, block):
        @pl.when(r + 1 < n_r if way == 0 else r > 0)
        def _():
            relay(*what, way, distance, block).start()

    forward(token_relay, 0, 0, r)
    forward(token_relay, 1, 0, r)

    row_id = lax.broadcasted_iota(jnp.int32, (IMAGES, 1), 0)
    image = lax.div(r * rows, PATCHES)
    resid = jnp.sum(x_all[r].astype(jnp.float32), axis=0, keepdims=True)
    mixed_all[r] = jnp.where(row_id == image, resid, 0.0) / PATCHES

    for k in range(1, n_q):
        stat_copy(k, peer_q(k)[0]).wait_recv()
    summed = stats[0]
    for k in range(1, n_q):
        summed = summed + stats[k]
    average = summed[0:1, :] / features
    variance = summed[1:2, :] / features - average * average
    spread = lax.rsqrt(variance + 1e-06)
    first = lax.broadcasted_iota(jnp.int32, (8, rows), 0) == 0
    row_stats[r] = jnp.where(first, average, spread)
    forward(rows_relay, 0, 0, r)
    forward(rows_relay, 1, 0, r)
    gain_copy.wait()

    partner = (g, r, c, os)
    across = (g, r, oc, s)

    def sub_copy(block, half, t):
        return pltpu.make_async_remote_copy(
            src_ref=to_sub.at[block, half, t], dst_ref=from_sub.at[block, half, t],
            send_sem=sub_send.at[block, half, t], recv_sem=sub_recv.at[block, half, t],
            device_id=partner, device_id_type=MESH)

    def col_copy(block, t):
        return pltpu.make_async_remote_copy(
            src_ref=to_col.at[block, t], dst_ref=from_col.at[block, t],
            send_sem=col_send.at[block, t], recv_sem=col_recv.at[block, t],
            device_id=across, device_id_type=MESH)

    def over_tiles(width, tile, body):
        def step(i, carry):
            body(pl.ds(pl.multiple_of(i * tile, 128), tile))
            return carry

        lax.fori_loop(0, width // tile, step, 0)

    def product(j, t):
        return jnp.dot(normed[...], w_in_v[j, t], preferred_element_type=jnp.float32)

    def process(block, mine):
        columns = jnp.transpose(jnp.concatenate([row_stats[block]] * 16, axis=0))
        mean_col, spread_col = columns[:, 0:1], columns[:, 1:2]

        def normalise(cols):
            values = x_all[block, :, cols].astype(jnp.float32)
            normed[:, cols] = (
                (values - mean_col) * spread_col * gain_v[:, cols]
            ).astype(jnp.bfloat16)

        over_tiles(depth, ct, normalise)

        def ready(j, t):
            @pl.when(mine)
            def _():
                w_in_copy(j, t).wait()

        def chip_sum(t):
            sub_copy(block, 0, t).wait_recv()
            to_col[block, t] = (
                kept[t] + from_sub[block, 0, t].astype(jnp.float32)
            ).astype(jnp.bfloat16)
            col_copy(block, t).start()

        def sent_quarters(t, carry):
            ready(0, t)
            to_sub[block, 0, t] = product(0, t).astype(jnp.bfloat16)
            sub_copy(block, 0, t).start()
            ready(1, t)
            kept[t] = product(1, t)

            @pl.when(t > 0)
            def _():
                chip_sum(t - 1)

            return carry

        def own_quarters(t, carry):
            ready(2, t)
            to_sub[block, 1, t] = product(2, t).astype(jnp.bfloat16)
            sub_copy(block, 1, t).start()

            @pl.when(t == 0)
            def _():
                chip_sum(tiles - 1)

            ready(3, t)
            own[block, t] = product(3, t)
            return carry

        lax.fori_loop(0, tiles, sent_quarters, 0)
        lax.fori_loop(0, tiles, own_quarters, 0)

        @pl.when(mine)
        def _():
            w_out_copy.start()
            captions_copy.start()

    def receive(distance):
        for what in (rows_relay, token_relay):
            @pl.when(r - distance >= 0)
            def _():
                relay_arrival(*what, 0, distance, r - distance).wait_recv()
                forward(what, 0, distance, r - distance)

            @pl.when(r + distance < n_r)
            def _():
                relay_arrival(*what, 1, distance, r + distance).wait_recv()
                forward(what, 1, distance, r + distance)

    def at_distance(distance, carry):
        @pl.when(distance > 0)
        def _():
            receive(distance)

        def side(which, inner):
            block = r + distance * (2 * which - 1)
            valid = (block >= 0) & (block < n_r) & ((distance > 0) | (which == 0))

            @pl.when(valid)
            def _():
                process(block, distance == 0)

            return inner

        lax.fori_loop(0, 2, side, 0)
        return carry

    lax.fori_loop(0, n_r, at_distance, 0)

    captions_copy.wait()
    norms = jnp.zeros((n_caps, 1), jnp.float32)
    for start in range(0, features, ct):
        part = captions_v[:, start : start + ct].astype(jnp.float32)
        norms += jnp.sum(part * part, axis=1, keepdims=True)
    text_scale = lax.rsqrt(norms / features + 1e-06)
    text_row = jnp.transpose(jnp.broadcast_to(text_scale, (n_caps, 128)))[0:1, :]

    b_in_copy.wait()
    b_out_copy.wait()
    pairs_copy.wait()
    pool_all[q] = jnp.zeros((tiles, IMAGES, ut), jnp.float32)
    acc_v[...] = jnp.zeros_like(acc_v)

    def finish(block, t):
        sub_copy(block, 1, t).wait_recv()
        col_copy(block, t).wait_recv()
        v = (
            own[block, t]
            + from_sub[block, 1, t].astype(jnp.float32)
            + from_col[block, t].astype(jnp.float32)
            + b_in_v[:, pl.ds(pl.multiple_of(t * ut, 128), ut)]
        )
        inner = 0.7978845608028654 * (v + 0.044715 * (v * v * v))
        hidden = (0.5 * v * (1.0 + jnp.tanh(inner))).astype(jnp.bfloat16)
        sums = jnp.sum(hidden.astype(jnp.float32), axis=0, keepdims=True)
        image_mask = row_id == lax.div(block * rows, PATCHES)
        pool_all[q, t] += jnp.where(image_mask, sums, 0.0)

    final = jnp.where(n_r - 1 - r >= r, n_r - 1, 0)

    def finish_distance(distance, carry):
        def side(which, inner):
            block = r + distance * (2 * which - 1)
            valid = (
                (block >= 0) & (block < n_r) & ((distance > 0) | (which == 0)) & (block != final)
            )

            @pl.when(valid)
            def _():
                def body(t, inside):
                    finish(block, t)
                    return inside

                lax.fori_loop(0, tiles, body, 0)

            return inner

        lax.fori_loop(0, 2, side, 0)
        return carry

    lax.fori_loop(0, n_r, finish_distance, 0)
    w_out_copy.wait()

    def pool_copy(k, t, slot):
        return q_copy(
            pool_all.at[slot, t], pool_all.at[slot, t], pool_send.at[k, t], pool_recv.at[k, t], k)

    def mix(t):
        for k in range(n_q):
            other = peer_q(k)[0]
            if k:
                pool_copy(k, t, other).wait_recv()
            value = pool_all[other, t] / PATCHES
            high = value.astype(jnp.bfloat16).astype(jnp.float32)
            rest = value - high
            middle = rest.astype(jnp.bfloat16).astype(jnp.float32)
            low = rest - middle
            terms = jnp.concatenate(
                [high, middle, low, jnp.zeros((8 - 3 * IMAGES, ut), jnp.float32)], axis=0
            ).astype(jnp.bfloat16)
            at = pl.ds(pl.multiple_of(other * units + t * ut, 128), ut)
            acc_v[...] += jnp.dot(terms, w_out_v[at, :], preferred_element_type=jnp.float32)

    def last_block(t, carry):
        @pl.when(t < tiles)
        def _():
            finish(final, t)
            for k in range(n_q - 1, 0, -1):
                pool_copy(k, t, q).start()

        @pl.when(t > 0)
        def _():
            mix(t - 1)

        return carry

    lax.fori_loop(0, tiles + 1, last_block, 0)
    acc = acc_v[...]
    mixed_all[r] = mixed_all[r] + (
        acc[0:IMAGES] + acc[IMAGES : 2 * IMAGES] + acc[2 * IMAGES : 3 * IMAGES]
    )

    def mixed_copy(k, slot):
        return pltpu.make_async_remote_copy(
            src_ref=mixed_all.at[slot], dst_ref=mixed_all.at[slot], send_sem=mixed_send.at[k],
            recv_sem=mixed_recv.at[slot], device_id=peer_r(k)[1], device_id_type=MESH)

    for k in range(1, n_r):
        mixed_copy(k, r).start()

    for k in range(1, n_q):
        stat_copy(k, q).wait_send()

    def drain(block, carry):
        def tile(t, inner):
            sub_copy(block, 0, t).wait_send()
            sub_copy(block, 1, t).wait_send()
            col_copy(block, t).wait_send()
            return inner

        lax.fori_loop(0, tiles, tile, 0)

        for what in (rows_relay, token_relay):
            @pl.when((block <= r) & (r + 1 < n_r))
            def _():
                relay(*what, 0, r - block, block).wait_send()

            @pl.when((block >= r) & (r > 0))
            def _():
                relay(*what, 1, block - r, block).wait_send()

        return carry

    lax.fori_loop(0, n_r, drain, 0)

    for k in range(1, n_q):
        for t in range(tiles):
            pool_copy(k, t, q).wait_send()

    for k in range(1, n_r):
        mixed_copy(k, peer_r(k)[0]).wait_recv()
    pooled = b_out_v[...] + mixed_all[0]
    for k in range(1, n_r):
        pooled = pooled + mixed_all[k]
    pooled_all[q] = pooled

    def pooled_copy(k, slot):
        return q_copy(
            pooled_all.at[slot], pooled_all.at[slot], pooled_send.at[k], pooled_recv.at[k], k)

    for k in range(n_q - 1, 0, -1):
        pooled_copy(k, q).start()
    power = jnp.zeros((IMAGES, 1), jnp.float32)
    similar = jnp.zeros((8, n_caps), jnp.float32)
    for k in range(n_q):
        other = peer_q(k)[0]
        if k:
            pooled_copy(k, other).wait_recv()
        value = pooled_all[other]
        power += jnp.sum(value * value, axis=1, keepdims=True)
        high = value.astype(jnp.bfloat16).astype(jnp.float32)
        terms = jnp.concatenate(
            [high, value - high, jnp.zeros((8 - 2 * IMAGES, depth), jnp.float32)], axis=0
        ).astype(jnp.bfloat16)
        similar += lax.dot_general(
            terms, captions_v[:, pl.ds(pl.multiple_of(other * depth, 128), depth)],
            (((1,), (1,)), ((), ())), preferred_element_type=jnp.float32)
    scale = lax.rsqrt(power / features + 1e-06)
    similar = (similar[0:IMAGES] + similar[IMAGES : 2 * IMAGES]) * scale
    chosen = pairs_v[...] == lax.broadcasted_iota(jnp.int32, (IMAGES, n_caps), 0)
    picked = jnp.sum(jnp.where(chosen, similar, 0.0), axis=0, keepdims=True)
    out_ref[...] = 100.0 * picked * text_row / features

    for k in range(1, n_q):
        pooled_copy(k, q).wait_send()
    for k in range(1, n_r):
        mixed_copy(k, r).wait_send()


def shards(shape, tokens, ln_gain, w_in, b_in, w_out, b_out, captions, pairs):
    n_r, n_c, n_s = shape["mrow"], shape["mcol"], shape["sub"]
    n_q = n_c * n_s
    rows, depth = tokens.shape
    units = w_in.shape[1] // n_q
    n_caps, features = captions.shape
    fits = (
        n_c == 2 and n_s == 2 and n_r > 1 and rows % 128 == 0 and PATCHES % rows == 0
        and depth % 128 == 0 and units % 128 == 0 and n_caps % 8 == 0
        and rows * n_r == IMAGES * PATCHES
    )
    if not fits:
        return plain(tokens, ln_gain, w_in, b_in, w_out, b_out, captions, pairs)
    ut = unit_tile(units)
    tiles = units // ut
    bf16, f32 = jnp.bfloat16, jnp.float32
    any_spec = pl.BlockSpec(memory_space=pl.ANY)
    vmem = pl.BlockSpec(memory_space=pltpu.VMEM)
    dma = pltpu.SemaphoreType.DMA
    result = pl.pallas_call(
        functools.partial(kernel, (n_r, n_c, n_s)),
        out_shape=jax.ShapeDtypeStruct((1, n_caps), f32),
        in_specs=[any_spec] * 8,
        out_specs=vmem,
        scratch_shapes=[
            pltpu.VMEM((n_r, rows, depth), bf16),
            pltpu.VMEM((rows, depth), bf16),
            pltpu.VMEM((4, tiles, depth, ut), bf16),
            pltpu.VMEM((w_out.shape[0], depth), bf16),
            pltpu.VMEM((n_caps, features), bf16),
            pltpu.VMEM((n_r, 2, tiles, rows, ut), bf16),
            pltpu.VMEM((n_r, 2, tiles, rows, ut), bf16),
            pltpu.VMEM((tiles, rows, ut), f32),
            pltpu.VMEM((n_r, tiles, rows, ut), bf16),
            pltpu.VMEM((n_r, tiles, rows, ut), bf16),
            pltpu.VMEM((n_r, tiles, rows, ut), f32),
            pltpu.VMEM((1, depth), f32),
            pltpu.VMEM((1, units), f32),
            pltpu.VMEM((1, depth), f32),
            pltpu.VMEM((1, n_caps), jnp.int32),
            pltpu.VMEM((n_q, 8, rows), f32),
            pltpu.VMEM((n_r, 8, rows), f32),
            pltpu.VMEM((n_q, tiles, IMAGES, ut), f32),
            pltpu.VMEM((8, depth), f32),
            pltpu.VMEM((n_r, IMAGES, depth), f32),
            pltpu.VMEM((n_q, IMAGES, depth), f32),
            dma((7,)), dma((4, tiles)),
            dma((2, n_r)), dma((2, n_r + 1)), dma((n_q,)), dma((n_q,)),
            dma((2, n_r)), dma((2, n_r + 1)),
            dma((n_r, 2, tiles)), dma((n_r, 2, tiles)), dma((n_r, tiles)), dma((n_r, tiles)),
            dma((n_q, tiles)), dma((n_q, tiles)), dma((n_r,)), dma((n_r,)),
            dma((n_q,)), dma((n_q,)),
        ],
        compiler_params=pltpu.CompilerParams(
            collective_id=0, has_side_effects=True, vmem_limit_bytes=66_000_000
        ),
        name="tower_scores",
    )(
        tokens, ln_gain[None, :], w_in, b_in[None, :], w_out, b_out[None, :], captions,
        pairs[None, :],
    )
    return result[0]


def solution(mesh):
    placed = (
        P(("group", "mrow"), ("mcol", "sub")),
        P(("mcol", "sub")),
        P(("mcol", "sub"), "mrow"),
        P("mrow"),
        P("mrow", ("mcol", "sub")),
        P(),
        P(("group", "mrow", "mcol", "sub"), None),
        P(("group", "mrow", "mcol", "sub")),
    )
    return jax.shard_map(
        functools.partial(shards, dict(mesh.shape)),
        mesh=mesh,
        in_specs=placed,
        out_specs=P(("group", "mrow", "mcol", "sub")),
        check_vma=False,
    )
```

```python
import functools

import jax
import jax.numpy as jnp
from jax import lax
from jax.experimental import pallas as pl
from jax.experimental.pallas import tpu as pltpu
from jax.sharding import PartitionSpec as P

MESH = pl.DeviceIdType.MESH

D = 6144
PATCHES = 256
IMAGES = 2


def image_table(first_row, count):
    positions = first_row + jnp.arange(count, dtype=jnp.int32)
    return (positions[None, :] // PATCHES == jnp.arange(IMAGES, dtype=jnp.int32)[:, None]).astype(
        jnp.bfloat16
    )


def plain(tokens, ln_gain, w_in, b_in, w_out, b_out, captions, pairs):
    values = tokens.astype(jnp.float32)
    totals, squares = lax.psum(
        (jnp.sum(values, axis=1), jnp.sum(values * values, axis=1)), ("mcol", "sub")
    )
    average = totals / D
    variance = squares / D - average * average
    normed = (
        (values - average[:, None]) * lax.rsqrt(variance + 1e-06)[:, None] * ln_gain[None, :]
    ).astype(jnp.bfloat16)
    gathered = lax.all_gather(normed, "mrow", axis=0, tiled=True)
    rows_local = tokens.shape[0]
    columns = tokens.shape[1]
    col_index = lax.axis_index(("mcol", "sub"))
    row_index = lax.axis_index("mrow")
    resid_pool = jnp.dot(
        image_table(row_index * rows_local, rows_local), tokens, preferred_element_type=jnp.float32
    )
    empty = jnp.zeros((IMAGES, D), jnp.float32)
    offset = col_index * columns
    out_weights = w_out.astype(jnp.float32)
    full_preact = jnp.dot(gathered, w_in, preferred_element_type=jnp.float32)
    preact = lax.psum_scatter(
        full_preact.astype(jnp.bfloat16), ("mcol", "sub"), scatter_dimension=1, tiled=True
    ).astype(jnp.float32)
    units = preact.shape[1]
    unit_bias = lax.dynamic_slice_in_dim(b_in, col_index * units, units, 0)
    hidden = jax.nn.gelu(preact + unit_bias[None, :], approximate=True).astype(jnp.bfloat16)
    local_pool = jnp.dot(
        image_table(0, hidden.shape[0]), hidden, preferred_element_type=jnp.float32
    )
    pooled_hidden = lax.all_gather(local_pool, ("mcol", "sub"), axis=1, tiled=True) / PATCHES
    mixed = jnp.dot(pooled_hidden, out_weights, precision=lax.Precision.HIGHEST)
    placed = lax.dynamic_update_slice(empty, resid_pool / PATCHES + mixed, (0, offset))
    pooled = lax.psum(placed, ("mrow", "mcol", "sub")) + b_out[None, :]
    embedding = (
        pooled * lax.rsqrt(jnp.mean(pooled * pooled, axis=1, keepdims=True) + 1e-06)
    ).astype(jnp.bfloat16)
    similar = jnp.dot(captions, embedding.T, preferred_element_type=jnp.float32)
    chosen = pairs[:, None] == jnp.arange(IMAGES, dtype=jnp.int32)[None, :]
    picked = jnp.sum(jnp.where(chosen, similar, 0.0), axis=1)
    text_vals = captions.astype(jnp.float32)
    text_scale = lax.rsqrt(jnp.mean(text_vals * text_vals, axis=1) + 1e-06)
    return 100.0 * picked * text_scale / D


def column_tile(width):
    return next(t for t in (1536, 768, 512, 384, 256, 128) if width % t == 0)


def unit_tile(width):
    return next(t for t in (512, 256, 384, 128) if width % t == 0)


def kernel(
    sizes,
    tokens_hbm, gain_hbm, w_in_hbm, b_in_hbm, w_out_hbm, b_out_hbm, captions_hbm, pairs_hbm,
    out_ref,
    x_all, normed, w_in_v, w_out_v, captions_v, captions_t, to_sub, from_sub, kept, to_col, from_col, own,
    gain_v, b_in_v, b_out_v, pairs_v, stats, row_stats, pool_all, acc_v, mixed_all, pooled_all,
    local_sem, w_sem,
    z_send, z_recv, stat_send, stat_recv, rows_send, rows_recv,
    sub_send, sub_recv, col_send, col_recv,
    pool_send, pool_recv, mixed_send, mixed_recv, pooled_send, pooled_recv,
):
    n_r, n_c, n_s = sizes
    n_q = n_c * n_s
    g = lax.axis_index("group")
    r = lax.axis_index("mrow")
    c = lax.axis_index("mcol")
    s = lax.axis_index("sub")
    oc, os = 1 - c, 1 - s
    q = c * n_s + s
    rows, depth = x_all.shape[1], x_all.shape[2]
    tiles, ut = own.shape[1], own.shape[3]
    units = tiles * ut
    features = depth * n_q
    n_caps = captions_v.shape[0]

    def peer_q(k):
        pc, ps = (oc if k & 2 else c), (os if k & 1 else s)
        return pc * n_s + ps, (g, r, pc, ps)

    def peer_r(k):
        other = lax.rem(r + k, n_r)
        return other, (g, other, c, s)

    quarters = (oc * n_s + os, oc * n_s + s, c * n_s + os, c * n_s + s)

    def w_in_copy(j, t):
        start = pl.multiple_of(quarters[j] * units + t * ut, 128)
        return pltpu.make_async_copy(
            w_in_hbm.at[:, pl.ds(start, ut)], w_in_v.at[j, t], w_sem.at[j, t])

    tokens_copy = pltpu.make_async_copy(tokens_hbm, x_all.at[r], local_sem.at[0])
    w_out_copy = pltpu.make_async_copy(w_out_hbm, w_out_v, local_sem.at[1])
    captions_copy = pltpu.make_async_copy(captions_hbm, captions_v, local_sem.at[2])
    gain_copy = pltpu.make_async_copy(gain_hbm, gain_v, local_sem.at[3])
    b_in_copy = pltpu.make_async_copy(
        b_in_hbm.at[:, pl.ds(pl.multiple_of(q * units, 128), units)], b_in_v, local_sem.at[4])
    b_out_copy = pltpu.make_async_copy(
        b_out_hbm.at[:, pl.ds(pl.multiple_of(q * depth, 128), depth)], b_out_v, local_sem.at[5])
    pairs_copy = pltpu.make_async_copy(pairs_hbm, pairs_v, local_sem.at[6])
    tokens_copy.start()

    barrier = pltpu.get_barrier_semaphore()
    for k in range(1, n_q):
        pl.semaphore_signal(barrier, inc=1, device_id=peer_q(k)[1], device_id_type=MESH)

    @pl.when(r > 0)
    def _():
        pl.semaphore_signal(barrier, inc=1, device_id=(g, r - 1, c, s), device_id_type=MESH)

    @pl.when(r + 1 < n_r)
    def _():
        pl.semaphore_signal(barrier, inc=1, device_id=(g, r + 1, c, s), device_id_type=MESH)

    gain_copy.start()
    tokens_copy.wait()
    w_in_copy(0, 0).start()
    w_in_copy(1, 0).start()

    ct = column_tile(depth)
    total = jnp.zeros((rows, 1), jnp.float32)
    squares = jnp.zeros((rows, 1), jnp.float32)
    for start in range(0, depth, ct):
        part = x_all[r, :, start : start + ct].astype(jnp.float32)
        total += jnp.sum(part, axis=1, keepdims=True)
        squares += jnp.sum(part * part, axis=1, keepdims=True)
    lane = lax.broadcasted_iota(jnp.int32, (rows, 128), 1)
    both = jnp.where(lane == 0, total, jnp.where(lane == 1, squares, 0.0))
    stats[q] = jnp.transpose(both)[:8, :]

    neighbours = jnp.where(r > 0, 1, 0) + jnp.where(r + 1 < n_r, 1, 0)
    pl.semaphore_wait(barrier, n_q - 1 + neighbours)

    def q_copy(src, dst, send, recv, k):
        return pltpu.make_async_remote_copy(
            src_ref=src, dst_ref=dst, send_sem=send, recv_sem=recv,
            device_id=peer_q(k)[1], device_id_type=MESH)

    def stat_copy(k, slot):
        return q_copy(stats.at[slot], stats.at[slot], stat_send.at[k], stat_recv.at[k], k)

    for k in range(n_q - 1, 0, -1):
        stat_copy(k, q).start()

    half_rows = rows // 2

    def relay(part, way, distance, block, to):
        if part == 2:
            ref, send, recv = row_stats.at[block], rows_send, rows_recv
        else:
            ref = x_all.at[block, pl.ds(part * half_rows, half_rows)]
            send, recv = z_send.at[part], z_recv.at[part]
        return pltpu.make_async_remote_copy(
            src_ref=ref, dst_ref=ref, send_sem=send.at[way, distance],
            recv_sem=recv.at[way, distance + 1], device_id=(g, to, c, s), device_id_type=MESH)

    def forward(part, way, distance, block):
        @pl.when(r + 1 < n_r if way == 0 else r > 0)
        def _():
            relay(part, way, distance, block, r + 1 if way == 0 else r - 1).start()

    for part in (0, 1):
        forward(part, 0, 0, r)
        forward(part, 1, 0, r)

    row_id = lax.broadcasted_iota(jnp.int32, (IMAGES, 1), 0)
    image = lax.div(r * rows, PATCHES)
    resid = jnp.sum(x_all[r].astype(jnp.float32), axis=0, keepdims=True)
    mixed_all[r] = jnp.where(row_id == image, resid, 0.0) / PATCHES

    for k in range(1, n_q):
        stat_copy(k, peer_q(k)[0]).wait_recv()
    for pair in (0, 2):
        for t in range(tiles):
            if pair + t > 0:
                w_in_copy(pair, t).start()
                w_in_copy(pair + 1, t).start()
    b_in_copy.start()
    b_out_copy.start()
    pairs_copy.start()
    summed = stats[0]
    for k in range(1, n_q):
        summed = summed + stats[k]
    average = summed[0:1, :] / features
    variance = summed[1:2, :] / features - average * average
    spread = lax.rsqrt(variance + 1e-06)
    first = lax.broadcasted_iota(jnp.int32, (8, rows), 0) == 0
    row_stats[r] = jnp.where(first, average, spread)
    forward(2, 0, 0, r)
    forward(2, 1, 0, r)
    gain_copy.wait()

    partner = (g, r, c, os)
    across = (g, r, oc, s)

    def sub_copy(block, half, t):
        return pltpu.make_async_remote_copy(
            src_ref=to_sub.at[block, half, t], dst_ref=from_sub.at[block, half, t],
            send_sem=sub_send.at[block, half, t], recv_sem=sub_recv.at[block, half, t],
            device_id=partner, device_id_type=MESH)

    def col_copy(block, t):
        return pltpu.make_async_remote_copy(
            src_ref=to_col.at[block, t], dst_ref=from_col.at[block, t],
            send_sem=col_send.at[block, t], recv_sem=col_recv.at[block, t],
            device_id=across, device_id_type=MESH)

    def over_tiles(width, tile, body):
        def step(i, carry):
            body(pl.ds(pl.multiple_of(i * tile, 128), tile))
            return carry

        lax.fori_loop(0, width // tile, step, 0)

    def product(j, t):
        return jnp.dot(normed[...], w_in_v[j, t], preferred_element_type=jnp.float32)

    def process(block, mine):
        columns = jnp.transpose(jnp.concatenate([row_stats[block]] * 16, axis=0))
        mean_col, spread_col = columns[:, 0:1], columns[:, 1:2]

        def normalise(cols):
            values = x_all[block, :, cols].astype(jnp.float32)
            normed[:, cols] = (
                (values - mean_col) * spread_col * gain_v[cols][None, :]
            ).astype(jnp.bfloat16)

        over_tiles(depth, ct, normalise)

        def ready(j, t):
            @pl.when(mine)
            def _():
                w_in_copy(j, t).wait()

        def chip_sum(t):
            sub_copy(block, 0, t).wait_recv()
            to_col[block, t] = (
                kept[t] + from_sub[block, 0, t].astype(jnp.float32)
            ).astype(jnp.bfloat16)
            col_copy(block, t).start()

        def sent_quarters(t, carry):
            ready(0, t)
            to_sub[block, 0, t] = product(0, t).astype(jnp.bfloat16)
            sub_copy(block, 0, t).start()
            ready(1, t)
            kept[t] = product(1, t)

            @pl.when(t > 0)
            def _():
                chip_sum(t - 1)

            return carry

        def own_quarters(t, carry):
            ready(2, t)
            to_sub[block, 1, t] = product(2, t).astype(jnp.bfloat16)
            sub_copy(block, 1, t).start()

            @pl.when(t == 0)
            def _():
                chip_sum(tiles - 1)

            ready(3, t)
            own[block, t] = product(3, t)
            return carry

        lax.fori_loop(0, tiles, sent_quarters, 0)
        lax.fori_loop(0, tiles, own_quarters, 0)

        @pl.when(mine)
        def _():
            w_out_copy.start()
            captions_copy.start()

    def receive(part, distance):
        @pl.when(r - distance >= 0)
        def _():
            relay(part, 0, distance - 1, r - distance, r).wait_recv()
            forward(part, 0, distance, r - distance)

        @pl.when(r + distance < n_r)
        def _():
            relay(part, 1, distance - 1, r + distance, r).wait_recv()
            forward(part, 1, distance, r + distance)

    def at_distance(distance, carry):
        @pl.when(distance > 0)
        def _():
            receive(1, distance)

        def side(which, inner):
            block = r + distance * (2 * which - 1)
            valid = (block >= 0) & (block < n_r) & ((distance > 0) | (which == 0))

            @pl.when(valid)
            def _():
                process(block, distance == 0)

            @pl.when(valid & ((which == 0) | (r < distance)))
            def _():
                receive(2, distance + 1)
                receive(0, distance + 1)

            return inner

        lax.fori_loop(0, 2, side, 0)
        return carry

    lax.fori_loop(0, n_r, at_distance, 0)

    captions_copy.wait()
    norms = jnp.zeros((n_caps, 1), jnp.float32)
    for start in range(0, features, ct):
        part = captions_v[:, start : start + ct].astype(jnp.float32)
        norms += jnp.sum(part * part, axis=1, keepdims=True)
        captions_t[start : start + ct, :] = jnp.transpose(part).astype(jnp.bfloat16)
    text_scale = lax.rsqrt(norms / features + 1e-06)
    text_row = jnp.transpose(jnp.broadcast_to(text_scale, (n_caps, 128)))[0:1, :]

    b_in_copy.wait()
    b_out_copy.wait()
    pairs_copy.wait()
    pool_all[q] = jnp.zeros((tiles, IMAGES, ut), jnp.float32)
    acc_v[...] = jnp.zeros_like(acc_v)

    def finish(block, t):
        sub_copy(block, 1, t).wait_recv()
        col_copy(block, t).wait_recv()
        v = (
            own[block, t]
            + from_sub[block, 1, t].astype(jnp.float32)
            + from_col[block, t].astype(jnp.float32)
            + b_in_v[:, pl.ds(pl.multiple_of(t * ut, 128), ut)]
        )
        inner = 0.7978845608028654 * (v + 0.044715 * (v * v * v))
        hidden = (0.5 * v * (1.0 + jnp.tanh(inner))).astype(jnp.bfloat16)
        sums = jnp.sum(hidden.astype(jnp.float32), axis=0, keepdims=True)
        image_mask = row_id == lax.div(block * rows, PATCHES)
        pool_all[q, t] += jnp.where(image_mask, sums, 0.0)

    final = jnp.where(n_r - 1 - r >= r, n_r - 1, 0)

    def finish_distance(distance, carry):
        def side(which, inner):
            block = r + distance * (2 * which - 1)
            valid = (
                (block >= 0) & (block < n_r) & ((distance > 0) | (which == 0)) & (block != final)
            )

            @pl.when(valid)
            def _():
                def body(t, inside):
                    finish(block, t)
                    return inside

                lax.fori_loop(0, tiles, body, 0)

            return inner

        lax.fori_loop(0, 2, side, 0)
        return carry

    lax.fori_loop(0, n_r, finish_distance, 0)
    w_out_copy.wait()

    def pool_copy(k, t, slot):
        return q_copy(
            pool_all.at[slot, t], pool_all.at[slot, t], pool_send.at[k, t], pool_recv.at[k, t], k)

    def mix(t):
        for k in range(n_q):
            other = peer_q(k)[0]
            if k:
                pool_copy(k, t, other).wait_recv()
            value = pool_all[other, t] / PATCHES
            high = value.astype(jnp.bfloat16).astype(jnp.float32)
            rest = value - high
            middle = rest.astype(jnp.bfloat16).astype(jnp.float32)
            low = rest - middle
            terms = jnp.concatenate(
                [high, middle, low, jnp.zeros((8 - 3 * IMAGES, ut), jnp.float32)], axis=0
            ).astype(jnp.bfloat16)
            at = pl.ds(pl.multiple_of(other * units + t * ut, 128), ut)
            acc_v[...] += jnp.dot(terms, w_out_v[at, :], preferred_element_type=jnp.float32)

    def last_block(t, carry):
        @pl.when(t < tiles)
        def _():
            finish(final, t)
            for k in range(n_q - 1, 0, -1):
                pool_copy(k, t, q).start()

        @pl.when(t > 0)
        def _():
            mix(t - 1)

        return carry

    lax.fori_loop(0, tiles + 1, last_block, 0)
    acc = acc_v[...]
    mixed_all[r] = mixed_all[r] + (
        acc[0:IMAGES] + acc[IMAGES : 2 * IMAGES] + acc[2 * IMAGES : 3 * IMAGES]
    )

    def mixed_copy(k, slot):
        return pltpu.make_async_remote_copy(
            src_ref=mixed_all.at[slot], dst_ref=mixed_all.at[slot], send_sem=mixed_send.at[k],
            recv_sem=mixed_recv.at[slot], device_id=peer_r(k)[1], device_id_type=MESH)

    for k in range(1, n_r):
        mixed_copy(k, r).start()

    for k in range(1, n_q):
        stat_copy(k, q).wait_send()

    def drain(block, carry):
        def tile(t, inner):
            sub_copy(block, 0, t).wait_send()
            sub_copy(block, 1, t).wait_send()
            col_copy(block, t).wait_send()
            return inner

        lax.fori_loop(0, tiles, tile, 0)

        for part in (0, 1, 2):
            @pl.when((block <= r) & (r + 1 < n_r))
            def _():
                relay(part, 0, r - block, block, r + 1).wait_send()

            @pl.when((block >= r) & (r > 0))
            def _():
                relay(part, 1, block - r, block, r - 1).wait_send()

        return carry

    lax.fori_loop(0, n_r, drain, 0)

    for k in range(1, n_q):
        for t in range(tiles):
            pool_copy(k, t, q).wait_send()

    for k in range(1, n_r):
        mixed_copy(k, peer_r(k)[0]).wait_recv()
    pooled = b_out_v[...] + mixed_all[0]
    for k in range(1, n_r):
        pooled = pooled + mixed_all[k]
    pooled_all[q] = pooled

    def pooled_copy(k, slot):
        return q_copy(
            pooled_all.at[slot], pooled_all.at[slot], pooled_send.at[k], pooled_recv.at[k], k)

    for k in range(n_q - 1, 0, -1):
        pooled_copy(k, q).start()
    power = jnp.zeros((IMAGES, 1), jnp.float32)
    similar = jnp.zeros((8, n_caps), jnp.float32)
    for k in range(n_q):
        other = peer_q(k)[0]
        if k:
            pooled_copy(k, other).wait_recv()
        value = pooled_all[other]
        power += jnp.sum(value * value, axis=1, keepdims=True)
        high = value.astype(jnp.bfloat16).astype(jnp.float32)
        terms = jnp.concatenate(
            [high, value - high, jnp.zeros((8 - 2 * IMAGES, depth), jnp.float32)], axis=0
        ).astype(jnp.bfloat16)
        similar += jnp.dot(
            terms, captions_t[pl.ds(pl.multiple_of(other * depth, 128), depth), :],
            preferred_element_type=jnp.float32)
    scale = lax.rsqrt(power / features + 1e-06)
    similar = (similar[0:IMAGES] + similar[IMAGES : 2 * IMAGES]) * scale
    chosen = pairs_v[...] == lax.broadcasted_iota(jnp.int32, (IMAGES, n_caps), 0)
    picked = jnp.sum(jnp.where(chosen, similar, 0.0), axis=0, keepdims=True)
    out_ref[...] = 100.0 * picked * text_row / features

    for k in range(1, n_q):
        pooled_copy(k, q).wait_send()
    for k in range(1, n_r):
        mixed_copy(k, r).wait_send()


def shards(shape, tokens, ln_gain, w_in, b_in, w_out, b_out, captions, pairs):
    n_r, n_c, n_s = shape["mrow"], shape["mcol"], shape["sub"]
    n_q = n_c * n_s
    rows, depth = tokens.shape
    units = w_in.shape[1] // n_q
    n_caps, features = captions.shape
    fits = (
        n_c == 2 and n_s == 2 and n_r > 1 and rows % 128 == 0 and PATCHES % rows == 0
        and depth % 128 == 0 and units % 128 == 0 and n_caps % 8 == 0
        and rows * n_r == IMAGES * PATCHES
    )
    if not fits:
        return plain(tokens, ln_gain, w_in, b_in, w_out, b_out, captions, pairs)
    ut = unit_tile(units)
    tiles = units // ut
    bf16, f32 = jnp.bfloat16, jnp.float32
    any_spec = pl.BlockSpec(memory_space=pl.ANY)
    vmem = pl.BlockSpec(memory_space=pltpu.VMEM)
    dma = pltpu.SemaphoreType.DMA
    result = pl.pallas_call(
        functools.partial(kernel, (n_r, n_c, n_s)),
        out_shape=jax.ShapeDtypeStruct((1, n_caps), f32),
        in_specs=[any_spec] * 8,
        out_specs=vmem,
        scratch_shapes=[
            pltpu.VMEM((n_r, rows, depth), bf16),
            pltpu.VMEM((rows, depth), bf16),
            pltpu.VMEM((4, tiles, depth, ut), bf16),
            pltpu.VMEM((w_out.shape[0], depth), bf16),
            pltpu.VMEM((n_caps, features), bf16),
            pltpu.VMEM((features, n_caps), bf16),
            pltpu.VMEM((n_r, 2, tiles, rows, ut), bf16),
            pltpu.VMEM((n_r, 2, tiles, rows, ut), bf16),
            pltpu.VMEM((tiles, rows, ut), f32),
            pltpu.VMEM((n_r, tiles, rows, ut), bf16),
            pltpu.VMEM((n_r, tiles, rows, ut), bf16),
            pltpu.VMEM((n_r, tiles, rows, ut), f32),
            pltpu.VMEM((depth,), f32),
            pltpu.VMEM((1, units), f32),
            pltpu.VMEM((1, depth), f32),
            pltpu.VMEM((1, n_caps), jnp.int32),
            pltpu.VMEM((n_q, 8, rows), f32),
            pltpu.VMEM((n_r, 8, rows), f32),
            pltpu.VMEM((n_q, tiles, IMAGES, ut), f32),
            pltpu.VMEM((8, depth), f32),
            pltpu.VMEM((n_r, IMAGES, depth), f32),
            pltpu.VMEM((n_q, IMAGES, depth), f32),
            dma((7,)), dma((4, tiles)),
            dma((2, 2, n_r)), dma((2, 2, n_r + 1)), dma((n_q,)), dma((n_q,)),
            dma((2, n_r)), dma((2, n_r + 1)),
            dma((n_r, 2, tiles)), dma((n_r, 2, tiles)), dma((n_r, tiles)), dma((n_r, tiles)),
            dma((n_q, tiles)), dma((n_q, tiles)), dma((n_r,)), dma((n_r,)),
            dma((n_q,)), dma((n_q,)),
        ],
        compiler_params=pltpu.CompilerParams(
            collective_id=0, has_side_effects=True, vmem_limit_bytes=66_000_000
        ),
        name="tower_scores",
    )(
        tokens, ln_gain, w_in, b_in[None, :], w_out, b_out[None, :], captions,
        pairs[None, :],
    )
    return result[0]


def solution(mesh):
    placed = (
        P(("group", "mrow"), ("mcol", "sub")),
        P(("mcol", "sub")),
        P(("mcol", "sub"), "mrow"),
        P("mrow"),
        P("mrow", ("mcol", "sub")),
        P(),
        P(("group", "mrow", "mcol", "sub"), None),
        P(("group", "mrow", "mcol", "sub")),
    )
    return jax.shard_map(
        functools.partial(shards, dict(mesh.shape)),
        mesh=mesh,
        in_specs=placed,
        out_specs=P(("group", "mrow", "mcol", "sub")),
        check_vma=False,
    )
```
